32 devices in a mesh: dp: 2 (over y), row: 4 (over x, core), col: 4 (over z).
Axes of the slice: x: 2, y: 2, z: 4, core: 2. Of those that a mesh axis runs over, the one named last changes fastest.
Arguments:
- block_input_rows: float32 [2048, 1024], P(('dp', 'row'), 'col'), may hold values from -6 to 6
- first_norm_gain: float32 [1024], P('col'), may hold values from 0.25 to 1.75
- in_weight: bfloat16 [3, 1024, 1024], P(None, 'col', 'row'), may hold values from -0.1875 to 0.1875
- conv_kernel: float32 [3, 1024], P(None, 'row'), may hold values from -3.5 to 3.5
- out_weight: bfloat16 [1024, 1024], P('row', 'col'), may hold values from -0.1875 to 0.1875
- second_norm_gain: float32 [1024], P('col'), may hold values from 0.25 to 1.75
- up_weights: bfloat16 [2, 1024, 4608], P(None, 'col', 'row'), may hold values from -0.1875 to 0.1875
- down_weight: bfloat16 [4608, 1024], P('row', 'col'), may hold values from -0.09375 to 0.09375
- segments: int32 [2048], P('dp'), may hold values from 0 to 4, never falling along the last dimension, each value on 1 to 1024 neighbouring positions
- cotangent: float32 [2048, 1024], P(('dp', 'row'), 'col'), may hold values from -6 to 6
Outputs:
- block_output: float32 [2048, 1024], P(('dp', 'row'), 'col')
- d_input: float32 [2048, 1024], P(('dp', 'row'), 'col')
- d_norm1_gain: float32 [1024], P('col')
- d_in_weight: float32 [3, 1024, 1024], P(None, 'col', 'row')
- d_conv_kernel: float32 [3, 1024], P(None, 'row')
- d_out_weight: float32 [1024, 1024], P('row', 'col')
- d_norm2_gain: float32 [1024], P('col')
- d_up_weights: float32 [2, 1024, 4608], P(None, 'col', 'row')
- d_down_weight: float32 [4608, 1024], P('row', 'col')
The draws below stay inside these ranges and needn't reach their ends.
Inputs may be any that keep to these rules, and one draw needn't show every extreme that they name: `segments`: segment numbers never fall along the tokens; a document holds at most 2000 tokens and at most half of all tokens, and some document reaches that bound.
All inputs are finite; a program needn't handle non-finite values.
Results may differ from the reference program's by a relative error of at most 0.009.
Values may be sent and summed in bfloat16 or wider, within the bound.
No kernel may reach another device: no remote copies, remote signals or barrier semaphores. Data moves between devices by JAX's collectives and lax.ppermute only.
A program may use at most 128 MiB of HBM per device.

```python
import math
import jax
import jax.numpy as jnp
import numpy as np
from jax import lax

MODEL_WIDTH = 1024
FF = 4608
KERNEL = 3
LENGTH = 1024
TOKENS = 2048


def block_scale(key, dims, split, least, top_value):
    level = 1.0
    for dim, parts in split:
        heights = jax.random.uniform(jax.random.fold_in(jax.random.fold_in(key, 6), dim), (parts,), jnp.float32, least / len(split), top_value / len(split))
        level = level * jnp.repeat(jnp.exp(heights), dims[dim] // parts).reshape((-1,) + (1,) * (len(dims) - 1 - dim))
    return level


def length_profile(number_of, total, most, slope):
    portions = [(1 << 20) // math.isqrt(standing ** slope) + 1 for standing in range(2, number_of + 1)]
    rest, holding = total - most - (number_of - 1), [1] * (number_of - 1)
    while rest > 0:
        candidates = [i for i in range(number_of - 1) if holding[i] < most]
        mass, budget = sum([portions[i] for i in candidates]), rest
        for i in candidates:
            addition = min(most - holding[i], max(1, budget * portions[i] // mass), rest)
            holding[i] = holding[i] + addition
            rest = rest - addition
    return np.array([most] + holding)


def uneven_parts(key, amount, total, most, lean):
    if amount == 2:
        one = jax.random.randint(key, (), max(1, total - most), min(most, total - 1) + 1)
        return jnp.stack([one, total - one])
    sizes = jnp.asarray(length_profile(amount, total, most, lean), jnp.int32)
    pairs = (amount - 1) // 2
    donor, taker = sizes[1:1 + 2 * pairs:2], sizes[2:2 + 2 * pairs:2]
    margin = jnp.minimum(donor - 1, most - taker)
    shifted = jax.random.randint(jax.random.fold_in(key, 1), (pairs,), 0, 1 << 20) % (margin + 1)
    sizes = sizes.at[1:1 + 2 * pairs:2].set(donor - shifted).at[2:2 + 2 * pairs:2].set(taker + shifted)
    return sizes[jax.random.permutation(jax.random.fold_in(key, 2), amount)]


def bell_draw(stream_key, shape, scale, bound, pieces=(), kind=jnp.bfloat16):
    entries = jax.random.normal(stream_key, shape, jnp.float32) * scale
    if len(pieces) > 0:
        entries = block_scale(stream_key, shape, pieces, -0.22, 0.18) * entries
    return jnp.clip(entries, min=-bound, max=bound).astype(kind)


def setup_inputs(seed: int = 0) -> dict:
    arg_keys = jax.random.split(jax.random.key(seed), 11)
    return {
        "block_input_rows": bell_draw(arg_keys[0], (TOKENS, MODEL_WIDTH), 1.0, 6.0, ((0, 8), (1, 4)), jnp.float32),
        "first_norm_gain": jnp.clip(1.0 + 0.15 * jax.random.normal(arg_keys[1], (MODEL_WIDTH,), jnp.float32), 0.25, 1.75),
        "in_weight": bell_draw(arg_keys[2], (3, MODEL_WIDTH, MODEL_WIDTH), MODEL_WIDTH ** -0.5, 0.1875, ((1, 4), (2, 4))),
        "conv_kernel": bell_draw(arg_keys[3], (KERNEL, MODEL_WIDTH), KERNEL ** -0.5, 3.5, ((1, 4),), jnp.float32),
        "out_weight": bell_draw(arg_keys[4], (MODEL_WIDTH, MODEL_WIDTH), MODEL_WIDTH ** -0.5, 0.1875, ((0, 4), (1, 4))),
        "second_norm_gain": jnp.clip(1.0 + 0.15 * jax.random.normal(arg_keys[5], (MODEL_WIDTH,), jnp.float32), 0.25, 1.75),
        "up_weights": bell_draw(arg_keys[6], (2, MODEL_WIDTH, FF), MODEL_WIDTH ** -0.5, 0.1875, ((1, 4), (2, 4))),
        "down_weight": bell_draw(arg_keys[7], (FF, MODEL_WIDTH), FF ** -0.5, 0.09375, ((0, 4), (1, 4))),
        "segments": jnp.searchsorted(jnp.cumsum(uneven_parts(arg_keys[8], max(4, TOKENS // 400), TOKENS, min(2000, TOKENS // 2), 0)), jnp.arange(TOKENS), side="right").astype(jnp.int32),
        "cotangent": bell_draw(arg_keys[9], (TOKENS, MODEL_WIDTH), 1.0, 6.0, ((0, 8), (1, 4)), jnp.float32),
    }


EPS = 1e-05

def lagged(value_rows, lag, fill):
    head = jnp.full((lag,) + value_rows.shape[1:], fill, value_rows.dtype)
    return jnp.concatenate([head, value_rows[:value_rows.shape[0] - lag]], axis=0)

def ahead(value_rows, lag):
    tail = jnp.zeros((lag,) + value_rows.shape[1:], value_rows.dtype)
    return jnp.concatenate([value_rows[lag:], tail], axis=0)

def mdot(left, right):
    return jnp.dot(left, right, preferred_element_type=jnp.float32)

def reference(block_input_rows, first_norm_gain, in_weight, conv_kernel, out_weight, second_norm_gain, up_weights, down_weight, segments, cotangent):
    kernel_len = conv_kernel.shape[0]
    width = block_input_rows.shape[1]
    count = block_input_rows.shape[0] // LENGTH
    inputs_seq = block_input_rows.reshape(count, LENGTH, width)
    cot_seq = cotangent.reshape(count, LENGTH, width)
    seg_seq = segments.reshape(count, LENGTH)

    def one_sequence(totals, inputs):
        input_rows, output_gradient, seg = inputs
        first_inverse_rms = lax.rsqrt(lax.optimization_barrier(jnp.mean(input_rows * input_rows, axis=1, keepdims=True)) + EPS)
        first_unit_scaled = input_rows * first_inverse_rms
        first_normalized = (first_unit_scaled * first_norm_gain).astype(jnp.bfloat16)
        bgate = mdot(first_normalized, in_weight[0])
        cgate = mdot(first_normalized, in_weight[1])
        xval = mdot(first_normalized, in_weight[2])
        bx = bgate * xval
        masks = [(seg == lagged(seg, lag, -1)).astype(jnp.float32)[:, None] for lag in range(kernel_len)]
        conv = jnp.zeros_like(bx)
        for lag in range(kernel_len):
            conv = conv + conv_kernel[kernel_len - 1 - lag] * lagged(bx, lag, 0.0) * masks[lag]
        mixed = (cgate * conv).astype(jnp.bfloat16)
        residual_stream = input_rows + mdot(mixed, out_weight)
        second_inverse_rms = lax.rsqrt(lax.optimization_barrier(jnp.mean(residual_stream * residual_stream, axis=1, keepdims=True)) + EPS)
        second_unit_scaled = residual_stream * second_inverse_rms
        second_normalized = (second_unit_scaled * second_norm_gain).astype(jnp.bfloat16)
        gate = mdot(second_normalized, up_weights[0])
        up = mdot(second_normalized, up_weights[1])
        sig = jax.nn.sigmoid(gate)
        act = (gate * sig * up).astype(jnp.bfloat16)
        output = residual_stream + mdot(act, down_weight)
        cot16 = output_gradient.astype(jnp.bfloat16)
        d_down = mdot(act.T, cot16)
        d_act = mdot(cot16, down_weight.T)
        d_gate = (d_act * up * sig * (1.0 + gate * (1.0 - sig))).astype(jnp.bfloat16)
        d_up = (d_act * gate * sig).astype(jnp.bfloat16)
        d_upw = jnp.stack([mdot(second_normalized.T, d_gate), mdot(second_normalized.T, d_up)])
        second_normalized_gradient = mdot(d_gate, up_weights[0].T) + mdot(d_up, up_weights[1].T)
        second_gain_gradient = lax.optimization_barrier(jnp.sum(second_normalized_gradient * second_unit_scaled, axis=0))
        second_gradient = second_normalized_gradient * second_norm_gain
        residual_gradient = output_gradient + second_inverse_rms * (second_gradient - second_unit_scaled * lax.optimization_barrier(jnp.mean(second_gradient * second_unit_scaled, axis=1, keepdims=True)))
        dres16 = residual_gradient.astype(jnp.bfloat16)
        d_outw = mdot(mixed.T, dres16)
        d_mixed = mdot(dres16, out_weight.T)
        d_cgate = d_mixed * conv
        d_conv = d_mixed * cgate
        kernel_rows = []
        for lag in range(kernel_len):
            kernel_rows.append(lax.optimization_barrier(jnp.sum(d_conv * lagged(bx, lag, 0.0) * masks[lag], axis=0)))
        d_kernel = jnp.stack(kernel_rows[::-1])
        d_bx = jnp.zeros_like(bx)
        for lag in range(kernel_len):
            d_bx = d_bx + conv_kernel[kernel_len - 1 - lag] * ahead(d_conv * masks[lag], lag)
        d_bgate = (d_bx * xval).astype(jnp.bfloat16)
        d_cg16 = d_cgate.astype(jnp.bfloat16)
        d_xval = (d_bx * bgate).astype(jnp.bfloat16)
        d_inw = jnp.stack([mdot(first_normalized.T, d_bgate), mdot(first_normalized.T, d_cg16), mdot(first_normalized.T, d_xval)])
        first_normalized_gradient = mdot(d_bgate, in_weight[0].T) + mdot(d_cg16, in_weight[1].T) + mdot(d_xval, in_weight[2].T)
        first_gain_gradient = lax.optimization_barrier(jnp.sum(first_normalized_gradient * first_unit_scaled, axis=0))
        first_gradient = first_normalized_gradient * first_norm_gain
        incoming_gradient = residual_gradient + first_inverse_rms * (first_gradient - first_unit_scaled * lax.optimization_barrier(jnp.mean(first_gradient * first_unit_scaled, axis=1, keepdims=True)))
        new_totals = (totals[0] + first_gain_gradient, totals[1] + d_inw, totals[2] + d_kernel, totals[3] + d_outw, totals[4] + second_gain_gradient, totals[5] + d_upw, totals[6] + d_down)
        return (new_totals, (output, incoming_gradient))
    start = (jnp.zeros(first_norm_gain.shape, jnp.float32), jnp.zeros(in_weight.shape, jnp.float32), jnp.zeros(conv_kernel.shape, jnp.float32), jnp.zeros(out_weight.shape, jnp.float32), jnp.zeros(second_norm_gain.shape, jnp.float32), jnp.zeros(up_weights.shape, jnp.float32), jnp.zeros(down_weight.shape, jnp.float32))
    totals, (outputs, d_inputs) = lax.scan(one_sequence, start, (inputs_seq, cot_seq, seg_seq))
    block_output = outputs.reshape(block_input_rows.shape)
    d_input = d_inputs.reshape(block_input_rows.shape)
    return (block_output, d_input, totals[0], totals[1], totals[2], totals[3], totals[4], totals[5], totals[6])
```

```python
import jax
import jax.numpy as jnp
from jax import lax
from jax.sharding import PartitionSpec as P

LENGTH = 1024
EPS = 1e-05
F32 = jnp.float32
BF16 = jnp.bfloat16


def inner_size():
    return 2 if lax.axis_size("row") % 2 == 0 else 1


def outer_size():
    return lax.axis_size("row") // inner_size()


def permute(value, axis, target):
    count = lax.axis_size(axis)
    return lax.ppermute(value, axis, [(source, target(source)) for source in range(count)])


def push(value, axis, step):
    count = lax.axis_size(axis)
    return permute(value, axis, lambda i: (i + step) % count)


def pull(value, axis, step):
    return push(value, axis, lax.axis_size(axis) - step)


def push_inner(value, step):
    inner = inner_size()
    return permute(value, "row", lambda i: i // inner * inner + (i % inner + step) % inner)


def push_outer(value, step):
    inner, outer = inner_size(), outer_size()
    return permute(value, "row", lambda i: (i // inner + step) % outer * inner + i % inner)


def pick(stacked, index):
    return lax.dynamic_index_in_dim(stacked, index, 0, keepdims=False)


def dot(left, right, contract):
    return lax.dot_general(left, right, (contract, ((), ())), preferred_element_type=F32)


def nn(left, right):
    return dot(left, right, ((1,), (0,)))


def nt(left, right):
    return dot(left, right, ((1,), (1,)))


def tn(left, right):
    return dot(left, right, ((0,), (0,)))


def gather_features(block):
    cols = lax.axis_size("col")
    return jnp.concatenate([block] + [pull(block, "col", k) for k in range(1, cols)], axis=-1)


def scatter_features(partial, extra=None):
    cols = lax.axis_size("col")
    width = partial.shape[1] // cols
    tokens = partial.shape[0]
    blocks = [lax.slice_in_dim(partial, k * width, (k + 1) * width, axis=1) for k in range(cols)]
    if extra is None:
        total = blocks[0]
        for k in range(1, cols):
            total = total + push(blocks[k].astype(BF16), "col", k).astype(F32)
        return total
    lines = -(-tokens // width)
    rows = jnp.pad(extra, (0, lines * width - tokens)).reshape(lines, width)
    rows = jnp.pad(rows, ((0, 16 - lines), (0, 0)))
    total, line_total = blocks[0], rows
    for k in range(1, cols):
        sent = jnp.concatenate([blocks[k], rows], axis=0).astype(BF16)
        got = push(sent, "col", k)
        total = total + got[:tokens].astype(F32)
        line_total = line_total + got[tokens:].astype(F32)
    return total, line_total[:lines].reshape(-1)[:tokens]


def spread_weights(block):
    cols = lax.axis_size("col")
    inner, outer = inner_size(), outer_size()
    planes, hidden, width = block.shape
    mine = lax.axis_index("col")
    pieces = jnp.moveaxis(block.reshape(planes, cols, hidden // cols, width), 1, 0)
    parts = [pick(pieces, mine)]
    for k in range(1, cols):
        parts.append(pull(pick(pieces, (mine - k) % cols), "col", k))
    own = jnp.concatenate(parts, axis=-1)
    line = [own] + [push_outer(own, outer - k) for k in range(1, outer)]
    if inner == 1:
        return line
    line = jnp.stack(line)
    return [line[k] for k in range(outer)] + [
        moved[k]
        for moved in [push_inner(line, inner - j) for j in range(1, inner)]
        for k in range(outer)
    ]


def local_slot(row):
    inner, outer = inner_size(), outer_size()
    me = lax.axis_index("row")
    return (row % inner - me % inner) % inner * outer + (row // inner - me // inner) % outer


def row_of_slot(slot):
    inner, outer = inner_size(), outer_size()
    me = lax.axis_index("row")
    return (me // inner + slot % outer) % outer * inner + (me % inner + slot // outer) % inner


def in_row_order(slices):
    stacked = jnp.stack(slices)
    return [pick(stacked, local_slot(jnp.int32(row))) for row in range(len(slices))]


def in_slot_order(stacked):
    return jnp.stack([pick(stacked, row_of_slot(slot)) for slot in range(stacked.shape[0])])


def collect_gradient(slices):
    cols, count = lax.axis_size("col"), lax.axis_size("dp")
    inner, outer = inner_size(), outer_size()
    mine, part = lax.axis_index("col"), lax.axis_index("dp")
    kept = slices[:outer].astype(F32)
    for j in range(1, inner):
        kept = kept + push_inner(slices[j * outer : (j + 1) * outer].astype(BF16), j).astype(F32)
    own = kept[0]
    for k in range(1, outer):
        own = own + push_outer(kept[k].astype(BF16), k).astype(F32)
    planes, hidden, full = own.shape
    width = full // cols
    split = jnp.moveaxis(own.reshape(planes, count, hidden // count, full), 1, 0)
    share = pick(split, part)
    for k in range(1, count):
        share = share + push(pick(split, (part + k) % count).astype(BF16), "dp", k).astype(F32)
    share = share.astype(BF16)
    got = [share[..., :width]]
    for k in range(1, cols):
        got.append(push(share[..., k * width : (k + 1) * width], "col", k))
    stacked = jnp.stack(got)
    block = jnp.stack([pick(stacked, (mine - c) % cols) for c in range(cols)])
    block = lax.optimization_barrier(block)
    both = jnp.stack([block] + [pull(block, "dp", k) for k in range(1, count)])
    both = jnp.stack([pick(both, (y - part) % count) for y in range(count)])
    return jnp.transpose(both, (2, 1, 0, 3, 4)).reshape(planes, cols * hidden, width)


def sum_rows(value):
    for axis in ("row", "dp"):
        count = lax.axis_size(axis)
        if count & (count - 1):
            value = lax.psum(value, axis)
            continue
        step = 1
        while step < count:
            value = value + permute(value, axis, lambda i: i ^ step)
            step *= 2
    return value


def per_device(
    block_input_rows,
    first_norm_gain,
    in_weight,
    conv_kernel,
    out_weight,
    second_norm_gain,
    up_weights,
    down_weight,
    segments,
    cotangent,
):
    rows, cols = lax.axis_size("row"), lax.axis_size("col")
    taps = conv_kernel.shape[0]
    halo = taps - 1
    tokens, width = block_input_rows.shape
    model_width = width * cols
    channels = conv_kernel.shape[1]
    channel_slice = channels // cols
    hidden_slice = up_weights.shape[2] // cols
    row, col = lax.axis_index("row"), lax.axis_index("col")

    start = row * tokens
    padded = jnp.concatenate(
        [jnp.full((halo,), -1, jnp.int32), segments, jnp.full((halo,), -2, jnp.int32)]
    )
    span = tokens + 2 * halo
    window = lax.dynamic_slice_in_dim(padded, start, span)
    positions = (start - halo + jnp.arange(span, dtype=jnp.int32)) % LENGTH

    def lag_mask(first, lag):
        base = first + halo
        current = lax.slice_in_dim(window, base, base + tokens)
        before = lax.slice_in_dim(window, base - lag, base - lag + tokens)
        place = lax.slice_in_dim(positions, base, base + tokens)
        return ((current == before) & (place >= lag)).astype(F32)[:, None]

    inputs_all = gather_features((block_input_rows * first_norm_gain).astype(BF16))
    gains = gather_features(jnp.stack([first_norm_gain, second_norm_gain]))
    first_gain, second_gain = gains[0], gains[1]
    mixer_block = jnp.concatenate([jnp.swapaxes(in_weight, 1, 2), out_weight[None]], axis=0)
    mixer = jnp.concatenate(in_row_order(spread_weights(mixer_block)), axis=1)
    in_all = mixer[:3].reshape(3 * rows * channel_slice, model_width)
    out_all = mixer[3]
    taps_own = lax.dynamic_slice_in_dim(conv_kernel, col * channel_slice, channel_slice, axis=1)
    kernel_rows = lax.all_gather(taps_own, "row", axis=1, tiled=True)
    cot_all = gather_features(cotangent.astype(BF16))
    pair_slices = spread_weights(jnp.swapaxes(up_weights, 1, 2))
    down_slices = spread_weights(down_weight[None])
    gate_all = jnp.concatenate([s[0] for s in pair_slices], axis=0)
    up_all = jnp.concatenate([s[1] for s in pair_slices], axis=0)
    down_all = jnp.concatenate([s[0] for s in down_slices], axis=0)

    def root_mean_square(scaled, gain):
        wide = scaled.astype(F32) / gain
        square = jnp.mean(wide * wide, axis=1, keepdims=True) + EPS
        return lax.rsqrt(square), jnp.sqrt(square)

    inverse1, rms1 = root_mean_square(inputs_all, first_gain)
    projected = nt(inputs_all, in_all) * inverse1
    lanes = rows * channel_slice
    bgate, cgate, xval = (projected[:, k * lanes : (k + 1) * lanes] for k in range(3))
    bx = bgate * xval
    edge = lax.ppermute(bx[tokens - halo :], "row", [(i, i + 1) for i in range(rows - 1)])
    bx_ext = jnp.concatenate([edge, bx], axis=0)
    masks = [lag_mask(0, lag) for lag in range(taps)]
    lagged_bx = [lax.slice_in_dim(bx_ext, halo - lag, halo - lag + tokens) for lag in range(taps)]
    conv = jnp.zeros_like(bx)
    for lag in range(taps):
        conv = conv + kernel_rows[taps - 1 - lag] * lagged_bx[lag] * masks[lag]
    mixed = (cgate * conv).astype(BF16)
    resid = block_input_rows + scatter_features(nn(mixed, out_all))

    resid_all = gather_features((resid * second_norm_gain).astype(BF16))
    inverse2, rms2 = root_mean_square(resid_all, second_gain)
    gate = nt(resid_all, gate_all) * inverse2
    upval = nt(resid_all, up_all) * inverse2
    sig = jax.nn.sigmoid(gate)
    act = (gate * sig * upval).astype(BF16)
    d_act = nt(cot_all, down_all) * inverse2
    d_gate = (d_act * upval * sig * (1.0 + gate * (1.0 - sig))).astype(BF16)
    d_up = (d_act * gate * sig).astype(BF16)
    d_normed2 = (nn(d_gate, gate_all) + nn(d_up, up_all)) * rms2
    inner2 = jnp.sum(d_normed2 * resid_all.astype(F32) * inverse2, axis=1)
    d_normed2, inner2 = scatter_features(d_normed2, inner2)
    block_output = resid + scatter_features(nn(act, down_all))

    own_unit2 = resid * inverse2
    d_resid = cotangent + inverse2 * (
        d_normed2 * second_norm_gain - own_unit2 * (inner2 / model_width)[:, None]
    )
    d_gain2 = jnp.sum(d_normed2 * own_unit2, axis=0)
    dres_all = gather_features(d_resid.astype(BF16))

    d_mixed = nt(dres_all, out_all)
    d_cgate = d_mixed * conv
    d_conv = d_mixed * cgate
    d_taps = [jnp.sum(d_conv * lagged_bx[lag] * masks[lag], axis=0) for lag in range(taps)]
    d_taps = jnp.stack(d_taps[::-1])
    after = lax.ppermute(d_conv[:halo], "row", [(i, i - 1) for i in range(1, rows)])
    conv_ext = jnp.concatenate([d_conv, after], axis=0)
    d_bx = jnp.zeros_like(d_conv)
    for lag in range(taps):
        d_bx = d_bx + kernel_rows[taps - 1 - lag] * lax.slice_in_dim(
            conv_ext, lag, lag + tokens
        ) * lag_mask(lag, lag)
    d_triple = jnp.concatenate([d_bx * xval, d_cgate, d_bx * bgate], axis=1)
    d_triple = (d_triple * inverse1).astype(BF16)
    d_normed1 = nn(d_triple, in_all) * rms1
    inner1 = jnp.sum(d_normed1 * inputs_all.astype(F32) * inverse1, axis=1)
    d_normed1, inner1 = scatter_features(d_normed1, inner1)
    own_unit1 = block_input_rows * inverse1
    d_input = d_resid + inverse1 * (
        d_normed1 * first_norm_gain - own_unit1 * (inner1 / model_width)[:, None]
    )
    d_gain1 = jnp.sum(d_normed1 * own_unit1, axis=0)

    def slots(gradient):
        return gradient.reshape(rows, 1, hidden_slice, model_width)

    d_down = collect_gradient(slots(tn(act, cot_all)))[0]
    d_pair = jnp.concatenate([slots(tn(d_gate, resid_all)), slots(tn(d_up, resid_all))], axis=1)
    d_pair = collect_gradient(d_pair)
    d_mixer = jnp.concatenate([tn(d_triple, inputs_all), tn(mixed, dres_all)], axis=0)
    d_mixer = jnp.moveaxis(d_mixer.reshape(4, rows, channel_slice, model_width), 1, 0)
    d_mixer = collect_gradient(in_slot_order(d_mixer))

    d_taps = sum_rows(d_taps).reshape(taps, rows, channel_slice)
    d_taps = lax.dynamic_index_in_dim(d_taps, row, 1, keepdims=False)
    d_taps = lax.all_gather(d_taps, "col", axis=1, tiled=True)
    d_gain1, d_gain2 = sum_rows(jnp.stack([d_gain1, d_gain2]))
    return (
        block_output,
        d_input,
        d_gain1,
        jnp.swapaxes(d_mixer[:3], 1, 2).astype(F32),
        d_taps,
        d_mixer[3].astype(F32),
        d_gain2,
        jnp.swapaxes(d_pair, 1, 2).astype(F32),
        d_down.astype(F32),
    )


def solution(mesh):
    return jax.shard_map(
        per_device,
        mesh=mesh,
        in_specs=(
            P(("dp", "row"), "col"),
            P("col"),
            P(None, "col", "row"),
            P(None, "row"),
            P("row", "col"),
            P("col"),
            P(None, "col", "row"),
            P("row", "col"),
            P("dp"),
            P(("dp", "row"), "col"),
        ),
        out_specs=(
            P(("dp", "row"), "col"),
            P(("dp", "row"), "col"),
            P("col"),
            P(None, "col", "row"),
            P(None, "row"),
            P("row", "col"),
            P("col"),
            P(None, "col", "row"),
            P("row", "col"),
        ),
        check_vma=False,
    )
```

```python
import jax
import jax.numpy as jnp
from jax import lax
from jax.sharding import PartitionSpec as P

LENGTH = 1024
EPS = 1e-05
F32 = jnp.float32
BF16 = jnp.bfloat16


def inner_size():
    return 2 if lax.axis_size("row") % 2 == 0 else 1


def outer_size():
    return lax.axis_size("row") // inner_size()


def permute(value, axis, target):
    count = lax.axis_size(axis)
    return lax.ppermute(value, axis, [(source, target(source)) for source in range(count)])


def push(value, axis, step):
    count = lax.axis_size(axis)
    return permute(value, axis, lambda i: (i + step) % count)


def pull(value, axis, step):
    return push(value, axis, lax.axis_size(axis) - step)


def push_inner(value, step):
    inner = inner_size()
    return permute(value, "row", lambda i: i // inner * inner + (i % inner + step) % inner)


def push_outer(value, step):
    inner, outer = inner_size(), outer_size()
    return permute(value, "row", lambda i: (i // inner + step) % outer * inner + i % inner)


def pick(stacked, index):
    return lax.dynamic_index_in_dim(stacked, index, 0, keepdims=False)


def dot(left, right, contract):
    return lax.dot_general(left, right, (contract, ((), ())), preferred_element_type=F32)


def nn(left, right):
    return dot(left, right, ((1,), (0,)))


def nt(left, right):
    return dot(left, right, ((1,), (1,)))


def tn(left, right):
    return dot(left, right, ((0,), (0,)))


def gather_features(block):
    cols = lax.axis_size("col")
    return jnp.concatenate([block] + [pull(block, "col", k) for k in range(1, cols)], axis=-1)


def scatter_features(partial, extra=None):
    cols = lax.axis_size("col")
    width = partial.shape[1] // cols
    tokens = partial.shape[0]
    blocks = [lax.slice_in_dim(partial, k * width, (k + 1) * width, axis=1) for k in range(cols)]
    if extra is None:
        total = blocks[0]
        for k in range(1, cols):
            total = total + push(blocks[k].astype(BF16), "col", k).astype(F32)
        return total
    lines = -(-tokens // width)
    rows = jnp.pad(extra, (0, lines * width - tokens)).reshape(lines, width)
    rows = jnp.pad(rows, ((0, 16 - lines), (0, 0)))
    total, line_total = blocks[0], rows
    for k in range(1, cols):
        sent = jnp.concatenate([blocks[k], rows], axis=0).astype(BF16)
        got = push(sent, "col", k)
        total = total + got[:tokens].astype(F32)
        line_total = line_total + got[tokens:].astype(F32)
    return total, line_total[:lines].reshape(-1)[:tokens]


def after(value, *earlier):
    return lax.optimization_barrier((value,) + earlier)[0]


def exchange_cols(block, shares, share):
    cols = lax.axis_size("col")
    hidden, width = block.shape[-2:]
    mine = lax.axis_index("col")
    pieces = block.reshape(block.shape[:-2] + (cols * shares, hidden // cols // shares, width))
    pieces = jnp.moveaxis(pieces, -3, 0)
    parts = [pick(pieces, mine * shares + share)]
    for k in range(1, cols):
        parts.append(pull(pick(pieces, (mine - k) % cols * shares + share), "col", k))
    return jnp.concatenate(parts, axis=-1)


def spread_outer(own):
    outer = outer_size()
    return jnp.stack([own] + [push_outer(own, outer - k) for k in range(1, outer)])


def spread_inner(near):
    inner = inner_size()
    return [near] + [push_inner(near, inner - j) for j in range(1, inner)]


def spread_dp(own):
    return jnp.stack([own] + [pull(own, "dp", k) for k in range(1, lax.axis_size("dp"))])


def spread_shared(own, outer_first):
    if outer_first:
        near = jnp.swapaxes(spread_dp(spread_outer(own)), 0, 1)
    else:
        near = spread_outer(spread_dp(own))
    return spread_inner(near.reshape(-1, own.shape[-1]))


def spread_slices(own):
    return [line[k] for line in spread_inner(spread_outer(own)) for k in range(outer_size())]


def local_slot(row):
    inner, outer = inner_size(), outer_size()
    me = lax.axis_index("row")
    return (row % inner - me % inner) % inner * outer + (row // inner - me // inner) % outer


def row_of_slot(slot):
    inner, outer = inner_size(), outer_size()
    me = lax.axis_index("row")
    return (me // inner + slot % outer) % outer * inner + (me % inner + slot // outer) % inner


def in_row_order(slices):
    stacked = jnp.stack(slices)
    return [pick(stacked, local_slot(jnp.int32(row))) for row in range(len(slices))]


def in_slot_order(stacked):
    return jnp.stack([pick(stacked, row_of_slot(slot)) for slot in range(stacked.shape[0])])


def collect_gradient(halves, planes, shared):
    cols, count = lax.axis_size("col"), lax.axis_size("dp")
    outer = outer_size()
    mine, part = lax.axis_index("col"), lax.axis_index("dp")
    kept = halves[0]
    for j in range(1, len(halves)):
        kept = kept + push_inner(halves[j].astype(BF16), j).astype(F32)
    full = kept.shape[-1]
    kept = kept.reshape(outer, planes, count, -1, full)
    own = kept[0]
    for k in range(1, outer):
        own = own + push_outer(kept[k].astype(BF16), k).astype(F32)
    split = jnp.moveaxis(own, 1, 0)
    if not shared:
        split = [pick(split, (part + k) % count) for k in range(count)]
    total = split[0]
    for k in range(1, count):
        total = total + push(split[k].astype(BF16), "dp", k).astype(F32)
    total = total.astype(BF16)
    width = full // cols
    got = [total[..., :width]]
    for k in range(1, cols):
        got.append(push(total[..., k * width : (k + 1) * width], "col", k))
    stacked = jnp.stack(got)
    block = jnp.stack([pick(stacked, (mine - c) % cols) for c in range(cols)])
    block = lax.optimization_barrier(block)
    both = jnp.stack([block] + [pull(block, "dp", k) for k in range(1, count)])
    both = jnp.stack([pick(both, (y - part) % count) for y in range(count)])
    return jnp.transpose(both, (2, 1, 0, 3, 4)).reshape(planes, -1, width)


def sum_rows(value):
    for axis in ("row", "dp"):
        count = lax.axis_size(axis)
        if count & (count - 1):
            value = lax.psum(value, axis)
            continue
        step = 1
        while step < count:
            value = value + permute(value, axis, lambda i: i ^ step)
            step *= 2
    return value


def per_device(
    block_input_rows,
    first_norm_gain,
    in_weight,
    conv_kernel,
    out_weight,
    second_norm_gain,
    up_weights,
    down_weight,
    segments,
    cotangent,
):
    rows, cols = lax.axis_size("row"), lax.axis_size("col")
    taps = conv_kernel.shape[0]
    halo = taps - 1
    tokens, width = block_input_rows.shape
    model_width = width * cols
    channels = conv_kernel.shape[1]
    channel_slice = channels // cols
    row, col = lax.axis_index("row"), lax.axis_index("col")

    start = row * tokens
    padded = jnp.concatenate(
        [jnp.full((halo,), -1, jnp.int32), segments, jnp.full((halo,), -2, jnp.int32)]
    )
    span = tokens + 2 * halo
    window = lax.dynamic_slice_in_dim(padded, start, span)
    positions = (start - halo + jnp.arange(span, dtype=jnp.int32)) % LENGTH

    def lag_mask(first, lag):
        base = first + halo
        current = lax.slice_in_dim(window, base, base + tokens)
        before = lax.slice_in_dim(window, base - lag, base - lag + tokens)
        place = lax.slice_in_dim(positions, base, base + tokens)
        return ((current == before) & (place >= lag)).astype(F32)[:, None]

    shares, share = lax.axis_size("dp"), lax.axis_index("dp")
    mixer_block = jnp.concatenate([jnp.swapaxes(in_weight, 1, 2), out_weight[None]], axis=0)
    mixer_own = exchange_cols(mixer_block, 1, 0)
    inputs_scaled = (block_input_rows * first_norm_gain).astype(BF16)
    inputs_all = gather_features(inputs_scaled)
    gains = gather_features(jnp.stack([first_norm_gain, second_norm_gain]))
    first_gain, second_gain = gains[0], gains[1]
    mixer = jnp.concatenate(in_row_order(spread_slices(mixer_own)), axis=1)
    in_all = mixer[:3].reshape(3 * rows * channel_slice, model_width)
    out_all = mixer[3]
    taps_own = lax.dynamic_slice_in_dim(conv_kernel, col * channel_slice, channel_slice, axis=1)
    kernel_rows = jnp.concatenate(in_row_order(spread_slices(taps_own)), axis=1)
    up_blocks = after(jnp.swapaxes(up_weights, 1, 2), inputs_all)
    gate_own = exchange_cols(up_blocks[0], shares, share)
    up_own = exchange_cols(up_blocks[1], shares, share)
    down_own = exchange_cols(after(down_weight, gate_own), shares, share)
    gate_halves = spread_shared(gate_own, True)
    up_halves = spread_shared(up_own, False)
    down_halves = spread_shared(down_own, True)
    cot_all = gather_features(after(cotangent.astype(BF16), up_own))

    def root_mean_square(scaled, gain):
        wide = scaled.astype(F32) / gain
        square = jnp.mean(wide * wide, axis=1, keepdims=True) + EPS
        return lax.rsqrt(square), jnp.sqrt(square)

    inverse1, rms1 = root_mean_square(inputs_all, first_gain)
    projected = nt(inputs_all, in_all) * inverse1
    lanes = rows * channel_slice
    bgate, cgate, xval = (projected[:, k * lanes : (k + 1) * lanes] for k in range(3))
    bx = bgate * xval
    edge = lax.ppermute(bx[tokens - halo :], "row", [(i, i + 1) for i in range(rows - 1)])
    bx_ext = jnp.concatenate([edge, bx], axis=0)
    masks = [lag_mask(0, lag) for lag in range(taps)]
    lagged_bx = [lax.slice_in_dim(bx_ext, halo - lag, halo - lag + tokens) for lag in range(taps)]
    conv = jnp.zeros_like(bx)
    for lag in range(taps):
        conv = conv + kernel_rows[taps - 1 - lag] * lagged_bx[lag] * masks[lag]
    mixed = (cgate * conv).astype(BF16)
    resid = block_input_rows + scatter_features(nn(mixed, out_all))

    resid_all = gather_features((resid * second_norm_gain).astype(BF16))
    inverse2, rms2 = root_mean_square(resid_all, second_gain)
    acts, d_gates, d_ups = [], [], []
    for gate_half, up_half, down_half in zip(gate_halves, up_halves, down_halves):
        gate = nt(resid_all, gate_half) * inverse2
        upval = nt(resid_all, up_half) * inverse2
        sig = jax.nn.sigmoid(gate)
        acts.append((gate * sig * upval).astype(BF16))
        d_act = nt(cot_all, down_half) * inverse2
        d_gates.append((d_act * upval * sig * (1.0 + gate * (1.0 - sig))).astype(BF16))
        d_ups.append((d_act * gate * sig).astype(BF16))
    d_normed2 = sum(nn(d, w) for d, w in zip(d_gates + d_ups, gate_halves + up_halves)) * rms2
    inner2 = jnp.sum(d_normed2 * resid_all.astype(F32) * inverse2, axis=1)
    d_normed2, inner2 = scatter_features(d_normed2, inner2)
    block_output = resid + scatter_features(sum(nn(a, w) for a, w in zip(acts, down_halves)))

    own_unit2 = resid * inverse2
    d_resid = cotangent + inverse2 * (
        d_normed2 * second_norm_gain - own_unit2 * (inner2 / model_width)[:, None]
    )
    d_gain2 = jnp.sum(d_normed2 * own_unit2, axis=0)
    dres_all = gather_features(d_resid.astype(BF16))

    d_mixed = nt(dres_all, out_all)
    d_cgate = d_mixed * conv
    d_conv = d_mixed * cgate
    d_taps = [jnp.sum(d_conv * lagged_bx[lag] * masks[lag], axis=0) for lag in range(taps)]
    d_taps = jnp.stack(d_taps[::-1])
    following = lax.ppermute(d_conv[:halo], "row", [(i, i - 1) for i in range(1, rows)])
    conv_ext = jnp.concatenate([d_conv, following], axis=0)
    d_bx = jnp.zeros_like(d_conv)
    for lag in range(taps):
        d_bx = d_bx + kernel_rows[taps - 1 - lag] * lax.slice_in_dim(
            conv_ext, lag, lag + tokens
        ) * lag_mask(lag, lag)
    d_triple = jnp.concatenate([d_bx * xval, d_cgate, d_bx * bgate], axis=1)
    d_triple = (d_triple * inverse1).astype(BF16)
    d_normed1 = nn(d_triple, in_all) * rms1
    inner1 = jnp.sum(d_normed1 * inputs_all.astype(F32) * inverse1, axis=1)
    d_normed1, inner1 = scatter_features(d_normed1, inner1)
    own_unit1 = block_input_rows * inverse1
    d_input = d_resid + inverse1 * (
        d_normed1 * first_norm_gain - own_unit1 * (inner1 / model_width)[:, None]
    )
    d_gain1 = jnp.sum(d_normed1 * own_unit1, axis=0)

    d_down = collect_gradient([tn(act, cot_all) for act in acts], 1, True)[0]
    d_gate = collect_gradient([tn(d, resid_all) for d in d_gates], 1, True)[0]
    d_up = collect_gradient([tn(d, resid_all) for d in d_ups], 1, True)[0]
    d_mixer = jnp.concatenate([tn(d_triple, inputs_all), tn(mixed, dres_all)], axis=0)
    d_mixer = jnp.moveaxis(d_mixer.reshape(4, rows, channel_slice, model_width), 1, 0)
    d_mixer = in_slot_order(d_mixer).reshape(inner_size(), -1, model_width)
    d_mixer = collect_gradient([d_mixer[j] for j in range(inner_size())], 4, False)

    d_taps = sum_rows(d_taps).reshape(taps, rows, channel_slice)
    d_taps = lax.dynamic_index_in_dim(d_taps, row, 1, keepdims=False)
    got_taps = jnp.stack([d_taps] + [pull(d_taps, "col", k) for k in range(1, cols)])
    d_taps = jnp.concatenate([pick(got_taps, (c - col) % cols) for c in range(cols)], axis=1)
    d_gain1, d_gain2 = sum_rows(jnp.stack([d_gain1, d_gain2]))
    return (
        block_output,
        d_input,
        d_gain1,
        jnp.swapaxes(d_mixer[:3], 1, 2).astype(F32),
        d_taps,
        d_mixer[3].astype(F32),
        d_gain2,
        jnp.stack([d_gate.T, d_up.T]).astype(F32),
        d_down.astype(F32),
    )


def solution(mesh):
    return jax.shard_map(
        per_device,
        mesh=mesh,
        in_specs=(
            P(("dp", "row"), "col"),
            P("col"),
            P(None, "col", "row"),
            P(None, "row"),
            P("row", "col"),
            P("col"),
            P(None, "col", "row"),
            P("row", "col"),
            P("dp"),
            P(("dp", "row"), "col"),
        ),
        out_specs=(
            P(("dp", "row"), "col"),
            P(("dp", "row"), "col"),
            P("col"),
            P(None, "col", "row"),
            P(None, "row"),
            P("row", "col"),
            P("col"),
            P(None, "col", "row"),
            P("row", "col"),
        ),
        check_vma=False,
    )
```

```python
import jax
import jax.numpy as jnp
from jax import lax
from jax.sharding import PartitionSpec as P


LENGTH = 1024
EPS = 1e-05
F32 = jnp.float32
BF16 = jnp.bfloat16


def inner_size():
    return 2 if lax.axis_size("row") % 2 == 0 else 1


def outer_size():
    return lax.axis_size("row") // inner_size()


def permute(value, axis, target):
    pairs = [(source, target(source)) for source in range(lax.axis_size(axis))]
    return lax.ppermute(value, axis, [pair for pair in pairs if pair[1] is not None])


def partner(index, step, count):
    return (index + step) % count if count & (count - 1) else index ^ step


def partnered(index, step, count):
    return (index - step) % count if count & (count - 1) else index ^ step


def step_to(index, other, count):
    return (other - index) % count if count & (count - 1) else index ^ other


def push(value, axis, step):
    count = lax.axis_size(axis)
    return permute(value, axis, lambda i: partner(i, step, count))


def pull(value, axis, step):
    count = lax.axis_size(axis)
    return permute(value, axis, lambda i: partnered(i, step, count))


def push_inner(value, step):
    inner = inner_size()
    return permute(value, "row", lambda i: i // inner * inner + (i % inner + step) % inner)


def push_outer(value, step):
    inner, outer = inner_size(), outer_size()
    return permute(value, "row", lambda i: (i // inner + step) % outer * inner + i % inner)


def pick(stacked, index):
    return lax.dynamic_index_in_dim(stacked, index, 0, keepdims=False)


def two_parts(value):
    high = lax.reduce_precision(value, 8, 7)
    return [high, lax.reduce_precision(value - high, 8, 7)]


def dot(left, right, contract):
    return lax.dot_general(left, right, (contract, ((), ())), preferred_element_type=F32)


def nn(left, right):
    return dot(left, right, ((1,), (0,)))


def nt(left, right):
    return dot(left, right, ((1,), (1,)))


def tn(left, right):
    return dot(left, right, ((0,), (0,)))


def gather_features(block, *gates):
    cols = lax.axis_size("col")
    moved = [after(pull(block, "col", k), *gates) for k in range(1, cols)]
    return jnp.concatenate([block] + moved, axis=-1)


def scatter_features(partial, extra=None, gates=()):
    cols = lax.axis_size("col")
    width = partial.shape[1] // cols
    tokens = partial.shape[0]
    blocks = [lax.slice_in_dim(partial, k * width, (k + 1) * width, axis=1) for k in range(cols)]
    if extra is None:
        total = blocks[0]
        for k in range(1, cols):
            got = after(push(blocks[k].astype(BF16), "col", k), *gates)
            total = total + got.astype(F32)
        return total
    lines = -(-tokens // width)
    rows = jnp.pad(extra, (0, lines * width - tokens)).reshape(lines, width)
    rows = jnp.pad(rows, ((0, 16 - lines), (0, 0)))
    total = jnp.concatenate([blocks[0], rows], axis=0)
    for k in range(1, cols):
        sent = jnp.concatenate([blocks[k], rows], axis=0).astype(BF16)
        total = total + after(push(sent, "col", k), *gates).astype(F32)
    return total[:tokens], total[tokens : tokens + lines].reshape(-1)[:tokens]


def after(value, *earlier):
    return lax.optimization_barrier((value,) + earlier)[0]


def marker(value):
    return lax.optimization_barrier(value * 3)


def exchange_cols(block, shares, share, gates=()):
    cols = lax.axis_size("col")
    hidden, width = block.shape[-2:]
    mine = lax.axis_index("col")
    pieces = block.reshape(block.shape[:-2] + (cols * shares, hidden // cols // shares, width))
    pieces = jnp.moveaxis(pieces, -3, 0)
    parts = [pick(pieces, mine * shares + share)]
    for k in range(1, cols):
        piece = pick(pieces, partnered(mine, k, cols) * shares + share)
        moved = pull(piece, "col", k)
        parts.append(after(moved, *gates))
    return jnp.concatenate(parts, axis=-1)


def spread_outer(own):
    outer = outer_size()
    return jnp.stack([own] + [push_outer(own, outer - k) for k in range(1, outer)])


def spread_inner(near):
    inner = inner_size()
    return [near] + [push_inner(near, inner - j) for j in range(1, inner)]


def spread_dp(own, *gates):
    count = lax.axis_size("dp")
    moved = [after(pull(own, "dp", k), *gates) for k in range(1, count)]
    return jnp.stack([own] + moved)


def spread_slices(own):
    lines = spread_inner(spread_outer(own))
    return [line[k] for line in lines for k in range(outer_size())]


def local_slot(row):
    inner, outer = inner_size(), outer_size()
    me = lax.axis_index("row")
    return (row % inner - me % inner) % inner * outer + (row // inner - me // inner) % outer


def row_of_slot(slot):
    inner, outer = inner_size(), outer_size()
    me = lax.axis_index("row")
    return (me // inner + slot % outer) % outer * inner + (me % inner + slot // outer) % inner


def in_row_order(slices):
    stacked = jnp.stack(slices)
    return [pick(stacked, local_slot(jnp.int32(row))) for row in range(len(slices))]


def in_slot_order(stacked):
    return jnp.stack([pick(stacked, row_of_slot(slot)) for slot in range(stacked.shape[0])])


def combine_inner(halves):
    kept = halves[0]
    for j in range(1, len(halves)):
        kept = kept + push_inner(halves[j].astype(BF16), j).astype(F32)
    return kept


def outer_parts(value):
    return [value[0]] + [value[k].astype(BF16) for k in range(1, value.shape[0])]


def dp_parts(value, shared):
    count, part = lax.axis_size("dp"), lax.axis_index("dp")
    value = jnp.moveaxis(value, -3, 0)
    shares = [value[k] if shared else pick(value, partner(part, k, count)) for k in range(count)]
    return shares[:1] + [each.astype(BF16) for each in shares[1:]]


def add_outer(parts, *gates):
    total = parts[0]
    for k in range(1, len(parts)):
        total = total + after(push_outer(parts[k], k), *gates).astype(F32)
    return total


def add_dp(parts, *gates):
    total = parts[0]
    for k in range(1, len(parts)):
        total = total + after(push(parts[k], "dp", k), *gates).astype(F32)
    return total


def own_columns(total, *gates):
    cols, mine = lax.axis_size("col"), lax.axis_index("col")
    total = total.astype(BF16)
    width = total.shape[-1] // cols
    got = [total[..., :width]]
    for k in range(1, cols):
        moved = push(total[..., k * width : (k + 1) * width], "col", k)
        got.append(after(moved, *gates))
    stacked = jnp.stack(got)
    return jnp.stack([pick(stacked, step_to(c, mine, cols)) for c in range(cols)])


def whole_gradient(block, *gates):
    count, part = lax.axis_size("dp"), lax.axis_index("dp")
    block = lax.optimization_barrier(block)
    moved = [after(pull(block, "dp", k), *gates) for k in range(1, count)]
    both = jnp.stack([block] + moved)
    both = jnp.stack([pick(both, step_to(part, y, count)) for y in range(count)], axis=1)
    both = jnp.moveaxis(both, (0, 1), (-4, -3))
    return both.reshape(both.shape[:-4] + (-1, both.shape[-1]))


def sum_rows(value):
    steps = []
    for axis in ("row", "dp"):
        count = lax.axis_size(axis)
        if count & (count - 1):
            value = lax.psum(value, axis)
        else:
            steps += [(axis, 1 << bit) for bit in range(count.bit_length() - 1)]
    first = [each for each in steps if each == ("row", 1)]
    dp = [each for each in steps if each[0] == "dp"]
    rest = [each for each in steps if each[0] == "row" and each[1] > 1]
    for axis, step in first + dp + rest:
        value = value + permute(value, axis, lambda i: i ^ step)
    return value


def per_device(
    block_input_rows,
    first_norm_gain,
    in_weight,
    conv_kernel,
    out_weight,
    second_norm_gain,
    up_weights,
    down_weight,
    segments,
    cotangent,
):
    rows, cols = lax.axis_size("row"), lax.axis_size("col")
    taps = conv_kernel.shape[0]
    halo = taps - 1
    tokens, width = block_input_rows.shape
    model_width = width * cols
    channels = conv_kernel.shape[1]
    channel_slice = channels // cols
    row, col = lax.axis_index("row"), lax.axis_index("col")

    start = row * tokens
    padded = jnp.concatenate(
        [jnp.full((halo,), -1, jnp.int32), segments, jnp.full((halo,), -2, jnp.int32)]
    )
    span = tokens + 2 * halo
    window = lax.dynamic_slice_in_dim(padded, start, span)
    positions = (start - halo + jnp.arange(span, dtype=jnp.int32)) % LENGTH

    def lag_mask(first, lag):
        base = first + halo
        current = lax.slice_in_dim(window, base, base + tokens)
        before = lax.slice_in_dim(window, base - lag, base - lag + tokens)
        place = lax.slice_in_dim(positions, base, base + tokens)
        return ((current == before) & (place >= lag)).astype(F32)[:, None]

    shares, share = lax.axis_size("dp"), lax.axis_index("dp")
    mixer_block = jnp.concatenate([jnp.swapaxes(in_weight, 1, 2), out_weight[None]], axis=0)
    planes = mixer_block.shape[0]
    weight_rows = planes * channel_slice
    taps_own = lax.dynamic_slice_in_dim(conv_kernel, col * channel_slice, channel_slice, axis=1)
    gain_rows = jnp.concatenate(two_parts(jnp.stack([first_norm_gain, second_norm_gain])))
    tap_rows = jnp.concatenate(two_parts(taps_own))
    tap_rows = jnp.pad(tap_rows, ((0, 0), (0, width - channel_slice)))
    extra_rows = -(-(4 + 2 * taps) // 16) * 16
    mixer_block = mixer_block.reshape(planes, cols, channel_slice, width)
    mixer_block = jnp.moveaxis(mixer_block, 1, 0).reshape(cols, weight_rows, width)
    more = jnp.concatenate([gain_rows, tap_rows]).astype(BF16)
    more = jnp.pad(more, ((0, extra_rows - more.shape[0]), (0, 0)))
    mixer_block = jnp.concatenate(
        [mixer_block, jnp.broadcast_to(more[None], (cols,) + more.shape)], axis=1
    )
    mixer_own = exchange_cols(mixer_block.reshape(-1, width), 1, 0)
    gains = mixer_own[weight_rows : weight_rows + 4].astype(F32)
    first_gain, second_gain = gains[0] + gains[2], gains[1] + gains[3]
    inputs_scaled = (block_input_rows * first_norm_gain).astype(BF16)
    inputs_all = gather_features(inputs_scaled)
    slices = in_row_order(spread_slices(mixer_own))
    mixer = jnp.concatenate(
        [piece[:weight_rows].reshape(planes, channel_slice, model_width) for piece in slices], axis=1
    )
    in_all = mixer[:3].reshape(3 * rows * channel_slice, model_width)
    out_all = mixer[3]
    tap_parts = jnp.concatenate([p[weight_rows + 4 :, :channel_slice] for p in slices], axis=1)
    tap_parts = tap_parts.astype(F32)
    kernel_rows = tap_parts[:taps] + tap_parts[taps : 2 * taps]

    def root_mean_square(scaled, gain):
        wide = scaled.astype(F32) / gain
        square = jnp.mean(wide * wide, axis=1, keepdims=True) + EPS
        return lax.rsqrt(square), jnp.sqrt(square)

    inverse1, rms1 = root_mean_square(inputs_all, first_gain)
    projected = nt(inputs_all, in_all) * inverse1
    lanes = rows * channel_slice
    bgate, cgate, xval = (projected[:, k * lanes : (k + 1) * lanes] for k in range(3))
    bx = bgate * xval
    edge = permute(bx[tokens - halo :], "row", lambda i: i + 1 if i + 1 < rows else None)
    bx_ext = jnp.concatenate([edge, bx], axis=0)
    masks = [lag_mask(0, lag) for lag in range(taps)]
    lagged_bx = [lax.slice_in_dim(bx_ext, halo - lag, halo - lag + tokens) for lag in range(taps)]
    conv = jnp.zeros_like(bx)
    for lag in range(taps):
        conv = conv + kernel_rows[taps - 1 - lag] * lagged_bx[lag] * masks[lag]
    mixed = (cgate * conv).astype(BF16)
    resid_part = nn(mixed, out_all)
    pair_own = exchange_cols(jnp.swapaxes(up_weights, 1, 2), shares, share, (mixer,))
    down_own = exchange_cols(down_weight, shares, share, (bx,))
    gate_line = spread_outer(pair_own[0])
    up_line = spread_dp(pair_own[1])
    down_line = spread_outer(down_own)
    cot_all = gather_features(cotangent.astype(BF16))
    mark = marker(segments)
    resid = block_input_rows + scatter_features(resid_part, gates=(mark,))

    resid_all = gather_features((resid * second_norm_gain).astype(BF16))
    inverse2, rms2 = root_mean_square(resid_all, second_gain)
    gate_near = jnp.swapaxes(spread_dp(gate_line), 0, 1).reshape(-1, model_width)
    up_near = spread_outer(up_line).reshape(-1, model_width)
    gate_halves = spread_inner(gate_near)
    up_halves = spread_inner(up_near)
    gates = [nt(resid_all, half) * inverse2 for half in gate_halves]
    ups = [nt(resid_all, half) * inverse2 for half in up_halves]
    down_near = spread_dp(down_line, gates[0], ups[0])
    down_near = jnp.swapaxes(down_near, 0, 1).reshape(-1, model_width)
    down_halves = spread_inner(down_near)
    acts, d_gates, d_ups = [], [], []
    for gate, upval, down_half in zip(gates, ups, down_halves):
        sig = jax.nn.sigmoid(gate)
        acts.append((gate * sig * upval).astype(BF16))
        d_act = nt(cot_all, down_half) * inverse2
        d_gates.append((d_act * upval * sig * (1.0 + gate * (1.0 - sig))).astype(BF16))
        d_ups.append((d_act * gate * sig).astype(BF16))
    d_normed2 = sum(nn(d, w) for d, w in zip(d_gates + d_ups, gate_halves + up_halves)) * rms2
    inner2 = jnp.sum(d_normed2 * resid_all.astype(F32) * inverse2, axis=1)
    down_kept = combine_inner([tn(act, cot_all) for act in acts])
    gate_kept = combine_inner([tn(d, resid_all) for d in d_gates])
    up_kept = combine_inner([tn(d, resid_all) for d in d_ups])
    by_slice = (outer_size(), shares, -1, model_width)
    down_parts = outer_parts(down_kept.reshape(by_slice))
    gate_parts = dp_parts(gate_kept.reshape(by_slice), True)
    up_parts = outer_parts(up_kept.reshape(by_slice))
    d_normed2, inner2 = scatter_features(d_normed2, inner2, (marker(after(segments, resid)),))
    own_unit2 = resid * inverse2
    d_resid = cotangent + inverse2 * (
        d_normed2 * second_norm_gain - own_unit2 * (inner2 / model_width)[:, None]
    )
    d_gain2 = jnp.sum(d_normed2 * own_unit2, axis=0)
    dres16 = d_resid.astype(BF16)
    dres_all = gather_features(dres16, up_parts[1])
    d_mixed = nt(dres_all, out_all)
    d_cgate = d_mixed * conv
    d_conv = d_mixed * cgate
    partial = sum(nn(after(a, dres16), w) for a, w in zip(acts, down_halves))
    block_output = resid + scatter_features(partial, gates=(d_conv,))

    d_taps = [jnp.sum(d_conv * lagged_bx[lag] * masks[lag], axis=0) for lag in range(taps)]
    d_taps = jnp.stack(d_taps[::-1])
    following = permute(d_conv[:halo], "row", lambda i: i - 1 if i else None)
    conv_ext = jnp.concatenate([d_conv, following], axis=0)
    d_bx = jnp.zeros_like(d_conv)
    for lag in range(taps):
        d_bx = d_bx + kernel_rows[taps - 1 - lag] * lax.slice_in_dim(
            conv_ext, lag, lag + tokens
        ) * lag_mask(lag, lag)
    d_triple = jnp.concatenate([d_bx * xval, d_cgate, d_bx * bgate], axis=1)
    d_triple = (d_triple * inverse1).astype(BF16)
    d_normed1 = nn(d_triple, in_all) * rms1
    inner1 = jnp.sum(d_normed1 * inputs_all.astype(F32) * inverse1, axis=1)
    triple, mixed_late = after(d_triple, d_normed1), after(mixed, d_normed1)
    d_mixer = jnp.concatenate([tn(triple, inputs_all), tn(mixed_late, dres_all)], axis=0)
    d_mixer = jnp.moveaxis(d_mixer.reshape(planes, rows, channel_slice, model_width), 1, 0)
    d_mixer = in_slot_order(d_mixer).reshape(inner_size(), -1, model_width)
    mix_kept = combine_inner([d_mixer[j] for j in range(inner_size())])
    mix_parts = outer_parts(mix_kept.reshape(outer_size(), planes, shares, -1, model_width))
    d_normed1, inner1 = scatter_features(d_normed1, inner1, (marker(after(segments, dres16)),))
    own_unit1 = block_input_rows * inverse1
    d_input = d_resid + inverse1 * (
        d_normed1 * first_norm_gain - own_unit1 * (inner1 / model_width)[:, None]
    )
    d_gain1 = jnp.sum(d_normed1 * own_unit1, axis=0)

    small = jnp.concatenate([d_taps, jnp.stack([d_gain1, d_gain2])])
    small = sum_rows(small)
    d_gain1, d_gain2 = small[taps], small[taps + 1]
    d_taps = small[:taps].reshape(taps, rows, channel_slice)
    d_taps = lax.dynamic_index_in_dim(d_taps, row, 1, keepdims=False)
    tap_rows = jnp.pad(jnp.concatenate(two_parts(d_taps)), ((0, 0), (0, width - channel_slice)))
    tap_rows = jnp.pad(tap_rows, ((0, extra_rows - 2 * taps), (0, 0)))

    down_parts = dp_parts(add_outer(down_parts, dres16), True)
    gate_total = add_outer(outer_parts(add_dp(gate_parts, dres16)), *mix_parts)
    down_total = add_dp(down_parts, *mix_parts)
    up_parts = dp_parts(add_outer(up_parts, *mix_parts), True)
    mix_parts = dp_parts(add_outer(mix_parts, up_parts[1]), False)
    mix_late = mix_parts
    first_two = jnp.stack([down_total, gate_total])
    first_two = own_columns(first_two, *mix_late)
    up_total = add_dp(up_parts)
    mix_total = add_dp(mix_parts, up_total)
    mix_rows = jnp.concatenate(
        [mix_total.reshape(-1, model_width), jnp.tile(tap_rows, (1, cols))]
    ).astype(BF16)
    d_up = own_columns(up_total, mix_rows)
    mix_block = own_columns(mix_rows)
    first_two = whole_gradient(first_two, mix_block)
    d_down, d_gate = first_two[0].astype(F32), first_two[1]
    d_up = whole_gradient(d_up)
    d_pair = jnp.stack([d_gate.T, d_up.T]).astype(F32)
    kept_rows = mix_total.size // model_width
    d_mixer = mix_block[:, :kept_rows].reshape(cols, planes, -1, width)
    d_mixer = whole_gradient(d_mixer, d_pair, d_down)
    tap_parts = mix_block[:, kept_rows:, :channel_slice].astype(F32)
    d_taps = tap_parts[:, :taps] + tap_parts[:, taps : 2 * taps]
    d_taps = jnp.moveaxis(d_taps, 1, 0).reshape(taps, channels)

    return (
        block_output,
        d_input,
        d_gain1,
        jnp.swapaxes(d_mixer[:3], 1, 2).astype(F32),
        d_taps,
        d_mixer[3].astype(F32),
        d_gain2,
        d_pair,
        d_down,
    )


def solution(mesh):
    return jax.shard_map(
        per_device,
        mesh=mesh,
        in_specs=(
            P(("dp", "row"), "col"),
            P("col"),
            P(None, "col", "row"),
            P(None, "row"),
            P("row", "col"),
            P("col"),
            P(None, "col", "row"),
            P("row", "col"),
            P("dp"),
            P(("dp", "row"), "col"),
        ),
        out_specs=(
            P(("dp", "row"), "col"),
            P(("dp", "row"), "col"),
            P("col"),
            P(None, "col", "row"),
            P(None, "row"),
            P("row", "col"),
            P("col"),
            P(None, "col", "row"),
            P("row", "col"),
        ),
        check_vma=False,
    )
```
